32 devices in a mesh: groups: 1, expert: 16 (over z, y, core), tensor: 2 (over x).
Axes of the slice: x: 2, y: 2, z: 4, core: 2. Of those that a mesh axis runs over, the one named last changes fastest.
Arguments:
- tokens: bfloat16 [2048, 4096], P(('groups', 'expert')), may hold values from -6 to 6
- expert_ids: int32 [2048, 8], P(('groups', 'expert')), may hold values from 0 to 15, all different within a row; in each aligned block of 128 rows (0 to 127, 128 to 255, ...) at most 96 rows name the same one
- route_weights: float32 [2048, 8], P(('groups', 'expert')), may hold values from 0.1 to 1
- gate_w: bfloat16 [16, 4096, 1536], P('expert', None, 'tensor'), may hold values from -0.09375 to 0.09375
- up_w: bfloat16 [16, 4096, 1536], P('expert', None, 'tensor'), may hold values from -0.09375 to 0.09375
- down_w: bfloat16 [16, 1536, 4096], P('expert', 'tensor'), may hold values from -0.15625 to 0.15625
Outputs:
- moe_out: bfloat16 [2048, 4096], P(('groups', 'expert'), 'tensor')
The draws below stay inside these ranges and needn't reach their ends.
Inputs may be any that keep to these rules, and one draw needn't show every extreme that they name: `expert_ids`: each row names 8 different experts. Among the rows of one device (aligned blocks of 128 rows) no expert is named more than 96 times, a bound that some block reaches.
All inputs are finite; a program needn't handle non-finite values.
Results may differ from the reference program's by a relative error of at most 0.014.
Values may be sent and summed in bfloat16 or wider, within the bound.
A program may use at most 128 MiB of HBM per device.

```python
import math
import jax
import jax.numpy as jnp
import numpy as np
from jax import lax

D = 4096
FF = 1536
TOK_DEV = 128
EXPERTS = 16
TOP = 8
CAP = 96
TOKENS = 2048


def block_levels(rng, extent, pieces, least, high):
    loudness, own = 1.0, jax.random.fold_in(rng, 6)
    for dim, shards_of in pieces:
        steps = jnp.exp(jax.random.uniform(jax.random.fold_in(own, dim), (shards_of,), jnp.float32, least / len(pieces), high / len(pieces)))
        loudness = loudness * jnp.repeat(steps, extent[dim] // shards_of).reshape([-1 if axis == dim else 1 for axis in range(len(extent))])
    return loudness


def routed_block(stream_key, own, number, rows, number_of, top, reach, slope):
    order = jax.random.permutation(stream_key, number_of)
    crowded, common = portions_of(number_of, rows * top, reach, slope, True), portions_of(number_of, rows * top, reach, slope, False)
    places = jnp.arange(number_of)

    def named(tallies, turn):
        used = int((tallies > 0).sum())
        fixed = max(1, used // 4)
        passed = fixed + (places - fixed + turn * (used - fixed)) % max(1, number_of - fixed)
        return jnp.zeros((number_of,), jnp.int32).at[order[jnp.where(places < fixed, places, passed)]].set(jnp.asarray(tallies, jnp.int32))

    tallies = jnp.where(number % 4 == 0, named(crowded, number // 4), named(common, number - number // 4 - 1))
    mixed = jax.random.permutation(jax.random.fold_in(own, 3), number_of)
    donor, sink = mixed[0:number_of // 2 * 2:2], mixed[1:number_of // 2 * 2:2]
    margin = jnp.minimum(tallies[donor] - 1, reach - tallies[sink]) // 2
    margin = jnp.where((donor == order[0]) | (sink == order[0]) | (tallies[sink] == 0), 0, jnp.maximum(margin, 0))
    passed = jax.random.randint(jax.random.fold_in(own, 4), (number_of // 2,), 0, 1 << 20) % (margin + 1)
    tallies = tallies.at[donor].add(-passed).at[sink].add(passed)
    members = jnp.searchsorted(jnp.cumsum(tallies), jnp.arange(rows * top), side="right").astype(jnp.int32)
    listing = members.reshape(top, rows).T
    listing = listing[jax.random.permutation(jax.random.fold_in(own, 1), rows)]
    turn = jax.random.randint(jax.random.fold_in(own, 2), (rows, 1), 0, top)
    return jnp.take_along_axis(listing, (jnp.arange(top)[None, :] + turn) % top, axis=1)


def portions_of(number_of, total, bound, slope, full):
    weights = [(1 << 20) // math.isqrt(grade ** slope) + 1 for grade in range(1, number_of + 1)]
    largest = bound if full else min(bound, max(-(-total // number_of), total * weights[0] // sum(weights)))
    least = 1 if total - largest >= number_of - 1 else 0
    holding, rest = [largest] + [least] * (number_of - 1), total - largest - least * (number_of - 1)
    while rest > 0:
        movable = [i for i in range(1, number_of) if holding[i] < largest] or [i for i in range(1, number_of) if holding[i] < bound]
        pool, remaining = sum([weights[i] for i in movable]), rest
        for i in movable:
            more = min(bound - holding[i], max(1, remaining * weights[i] // pool), rest)
            holding[i] = holding[i] + more
            rest = rest - more
    return np.array(holding)


def normal_values(stream_key, shape, spread, most, shards=(), kind=jnp.bfloat16):
    values = spread * jax.random.normal(stream_key, shape, jnp.float32)
    if shards:
        values = values * block_levels(stream_key, shape, shards, -0.22, 0.18)
    return jnp.clip(values, -most, most).astype(kind)


def setup_inputs(seed: int = 0, part: int = 0) -> dict:
    splits = jax.random.split(jax.random.key(seed), 7)
    own_keys = jax.random.split(jax.random.fold_in(splits[6], part), 7)
    tokens = normal_values(own_keys[0], (TOKENS, D), 1.0, 6.0, ((0, 16),))
    expert_ids_keys = jax.random.split(jax.random.fold_in(own_keys[1], 1), TOKENS // TOK_DEV)
    expert_ids_turns = jax.random.permutation(jax.random.fold_in(own_keys[1], 3), TOKENS // TOK_DEV)
    expert_ids = jax.vmap(lambda own, number: routed_block(jax.random.fold_in(own_keys[1], 2), own, number, TOK_DEV, EXPERTS, TOP, CAP, 2))(expert_ids_keys, expert_ids_turns).reshape((TOKENS, TOP))
    route_weights = jnp.clip(0.1 + 0.9 * jax.random.uniform(own_keys[2], (TOKENS, TOP), jnp.float32) ** block_levels(own_keys[2], (TOKENS, TOP), ((0, 16),), -0.2, 0.2), 0.1, 1.0)
    gate_w = normal_values(splits[3], (EXPERTS, D, FF), D ** -0.5, 0.09375, ((0, 16), (2, 2)))
    up_w = normal_values(splits[4], (EXPERTS, D, FF), D ** -0.5, 0.09375, ((0, 16), (2, 2)))
    down_w = normal_values(splits[5], (EXPERTS, FF, D), FF ** -0.5, 0.15625, ((0, 16), (1, 2)))
    return dict(tokens=tokens, expert_ids=expert_ids, route_weights=route_weights, gate_w=gate_w, up_w=up_w, down_w=down_w)


def reference(tokens, expert_ids, route_weights, gate_w, up_w, down_w):
    total_rows = tokens.shape[0]
    blocks = total_rows // TOK_DEV
    grouped = expert_ids.reshape(blocks, TOK_DEV * TOP)
    onehot = (grouped[:, :, None] == jnp.arange(EXPERTS, dtype=jnp.int32)[None, None, :]).astype(jnp.int32)
    before = jnp.cumsum(onehot, axis=1) - onehot
    slot = jnp.sum(before * onehot, axis=2)
    block_index = jnp.arange(blocks, dtype=jnp.int32)[:, None]
    position = (block_index * CAP + slot).reshape(-1).astype(jnp.int32)
    flat_ids = expert_ids.reshape(-1)
    flat_weights = route_weights.reshape(-1)
    token_index = (jnp.arange(total_rows * TOP, dtype=jnp.int32) // TOP).astype(jnp.int32)
    quarter = FF // 4
    outside = blocks * CAP

    def step(accum, expert):
        chosen = flat_ids == expert
        target = jnp.where(chosen, position, outside).astype(jnp.int32)
        source = jnp.zeros((outside,), jnp.int32).at[target].set(token_index, mode="drop")
        filled = jnp.zeros((outside,), jnp.bool_).at[target].set(True, mode="drop")
        rows = jnp.where(filled[:, None], tokens[source], jnp.zeros((), tokens.dtype))
        gate = jnp.dot(rows, gate_w[expert], preferred_element_type=jnp.float32)
        up_part = jnp.dot(rows, up_w[expert], preferred_element_type=jnp.float32)
        hidden = (jax.nn.silu(gate) * up_part).astype(jnp.bfloat16)
        summed = jnp.zeros((outside, D), jnp.float32)
        for block in range(4):
            piece = jnp.dot(hidden[:, block * quarter:(block + 1) * quarter],
                            down_w[expert][block * quarter:(block + 1) * quarter],
                            preferred_element_type=jnp.float32).astype(jnp.bfloat16)
            piece = lax.optimization_barrier(piece)
            summed = summed + piece.astype(jnp.float32)
        expert_out = summed.astype(jnp.bfloat16)
        weight_pick = jnp.where(chosen, flat_weights, jnp.zeros((), flat_weights.dtype)).reshape(total_rows, TOP)
        where_rows = jnp.where(chosen, position, 0).astype(jnp.int32).reshape(total_rows, TOP)
        for choice_index in range(TOP):
            fetched = expert_out[where_rows[:, choice_index]].astype(jnp.float32)
            accum = accum + weight_pick[:, choice_index][:, None].astype(jnp.float32) * fetched
        return accum, None

    start = jnp.zeros((total_rows, D), jnp.float32)
    result, unused = lax.scan(step, start, jnp.arange(EXPERTS, dtype=jnp.int32))
    return result.astype(jnp.bfloat16)
```

```python
import functools

import jax
import jax.numpy as jnp
from jax import lax
from jax.experimental import pallas as pl
from jax.experimental.pallas import tpu as pltpu
from jax.sharding import PartitionSpec as P

MESH = pl.DeviceIdType.MESH
F32, BF16 = jnp.float32, jnp.bfloat16
ORDER = (
    (0, 2, 1, 4, 3, 6, 5, 7),
    (2, 0, 3, 4, 1, 6, 5, 7),
    (4, 6, 5, 2, 7, 0, 3, 1),
    (6, 4, 7, 2, 5, 0, 3, 1),
)
TARGETS = (3, 0, 2, 1)


def place():
    e = lax.axis_index("expert")
    return e, e // 4, (e // 2) % 2, e % 2, lax.axis_index("tensor")


def pick(index, values):
    out = jnp.int32(0)
    for k, v in enumerate(values):
        if v:
            out = out + jnp.where(index == k, jnp.int32(v), jnp.int32(0))
    return out


def dev(z, y, c, x):
    return {"expert": (z * 2 + y) * 2 + c, "tensor": x}


def gather_kernel(
    tok, wts, gate_hbm, up_hbm, hid, held, gate_v, up_v, wall,
    own_sem, load_sem, wsend, wrecv, zs, ys, xs, cs, cxs, rp, rx, rc, rcx,
):
    e, z, y, c, x = place()
    n_dev = wall.shape[0]
    rows = held.shape[1]
    lane = 3 * rows // 8
    main = rows - lane
    mine = pl.ds(pl.multiple_of(lane * x, 16), main)
    out_x = pl.ds(pl.multiple_of(main * x, 16), lane)
    in_x = pl.ds(pl.multiple_of(main * (1 - x), 16), lane)
    me_q = z * 2 + y

    load_own = pltpu.make_async_copy(tok, held.at[e], own_sem.at[0])
    load_own.start()
    load_gate = pltpu.make_async_copy(gate_hbm.at[0], gate_v, load_sem.at[0])
    load_up = pltpu.make_async_copy(up_hbm.at[0], up_v, load_sem.at[1])
    load_gate.start()
    load_up.start()
    load_w = pltpu.make_async_copy(wts, wall.at[e], own_sem.at[1])
    load_w.start()

    barrier = pltpu.get_barrier_semaphore()

    def greet(k, carry):
        pl.semaphore_signal(
            barrier, inc=1, device_id={"expert": (e + k) % n_dev, "tensor": x}, device_id_type=MESH
        )
        return carry

    lax.fori_loop(1, n_dev, greet, 0)
    pl.semaphore_signal(barrier, inc=1, device_id=dev(z, y, c, 1 - x), device_id_type=MESH)
    pl.semaphore_wait(barrier, n_dev)

    def cp(q, lane_c, part, send, recv, target):
        ref = held.at[q * 2 + lane_c] if part is None else held.at[q * 2 + lane_c, part]
        return pltpu.make_async_remote_copy(
            src_ref=ref, dst_ref=ref, send_sem=send, recv_sem=recv,
            device_id=target, device_id_type=MESH,
        )

    def up_copy(q):
        return cp(q, c, mine, zs.at[0, q // 2], rp.at[q], dev(jnp.minimum(z + 1, 3), y, c, x))

    def down_copy(q):
        return cp(q, c, mine, zs.at[1, q // 2], rp.at[q], dev(jnp.maximum(z - 1, 0), y, c, x))

    def y_copy(q):
        return cp(q, c, mine, ys.at[q // 2], rp.at[q], dev(z, 1 - y, c, x))

    def x_copy(q):
        return cp(q, c, out_x, xs.at[q], rx.at[q], dev(z, y, c, 1 - x))

    def x_arrive(q):
        return cp(q, c, in_x, xs.at[q], rx.at[q], dev(z, y, c, 1 - x))

    def core_copy(q, lane_c):
        return cp(q, lane_c, mine, cs.at[q], rc.at[q], dev(z, y, 1 - c, x))

    def core_x_copy(q, lane_c):
        return cp(q, lane_c, in_x, cxs.at[q], rcx.at[q], dev(z, y, 1 - c, x))

    def w_copy(k):
        return pltpu.make_async_remote_copy(
            src_ref=wall.at[e], dst_ref=wall.at[e], send_sem=wsend.at[k], recv_sem=wrecv.at[k],
            device_id={"expert": (e + k) % n_dev, "tensor": x}, device_id_type=MESH,
        )

    def w_arrive(k):
        ref = wall.at[(e + n_dev - k) % n_dev]
        return pltpu.make_async_remote_copy(
            src_ref=ref, dst_ref=ref, send_sem=wsend.at[k], recv_sem=wrecv.at[k],
            device_id={"expert": (e + k) % n_dev, "tensor": x}, device_id_type=MESH,
        )

    load_own.wait()

    @pl.when(z < 3)
    def _():
        up_copy(me_q).start()

    @pl.when(z > 0)
    def _():
        down_copy(me_q).start()

    y_copy(me_q).start()
    core_copy(me_q, c).start()
    core_x_copy(me_q, c).start()
    load_w.wait()

    def send_w(k, carry):
        w_copy(k).start()
        return carry

    lax.fori_loop(1, n_dev, send_w, 0)

    def entry(j):
        v = pick(z * 8 + j, [v for row in ORDER for v in row])
        own_y = v % 2 == 0
        return (v // 2) * 2 + jnp.where(own_y, y, 1 - y), v // 2, own_y

    def compute(q):
        a = held[pl.ds(q * 2, 2)].reshape(2 * rows, held.shape[2])
        experts = wall.shape[1]
        col = lax.broadcasted_iota(jnp.int32, (rows, experts), 1) == e
        w0 = jnp.sum(jnp.where(col, wall[q * 2].T, 0.0), axis=1, keepdims=True)
        w1 = jnp.sum(jnp.where(col, wall[q * 2 + 1].T, 0.0), axis=1, keepdims=True)
        w = jnp.concatenate([w0, w1], axis=0)
        for n in range(0, gate_v.shape[1], 256):
            g = jnp.dot(a, gate_v[:, n:n + 256], preferred_element_type=F32)
            u = jnp.dot(a, up_v[:, n:n + 256], preferred_element_type=F32)
            h = (g / (1.0 + jnp.exp(-g)) * u * w).astype(BF16)
            hid[pl.ds(q * 2, 2), :, n:n + 256] = h.reshape(2, rows, 256)

    def step(j, carry):
        @pl.when((j >= 1) & (j < 8))
        def _():
            q, zz, own_y = entry(j)
            y_copy(q).wait_recv()

            @pl.when(own_y & (zz < z) & (z < 3))
            def _():
                up_copy(q).start()

            @pl.when(own_y & (zz > z) & (z > 0))
            def _():
                down_copy(q).start()

            @pl.when(own_y)
            def _():
                y_copy(q).start()

            x_copy(q).start()
            core_copy(q, c).start()

        @pl.when((j >= 2) & (j < 9))
        def _():
            q, zz, own_y = entry(j - 1)
            x_arrive(q).wait_recv()
            core_x_copy(q, c).start()

        @pl.when(j == 0)
        def _():
            load_gate.wait()
            load_up.wait()

            def got_w(k, carry):
                w_arrive(k).wait_recv()
                return carry

            lax.fori_loop(1, n_dev, got_w, 0)

        @pl.when((j == 0) | (j >= 3))
        def _():
            q, zz, own_y = entry(jnp.where(j == 0, 0, j - 2))
            core_copy(q, 1 - c).wait_recv()
            core_x_copy(q, 1 - c).wait_recv()
            compute(q)

        return carry

    lax.fori_loop(0, 10, step, 0)

    def drain_w(k, carry):
        w_copy(k).wait_send()
        return carry

    lax.fori_loop(1, n_dev, drain_w, 0)

    def drain(j, carry):
        q, zz, own_y = entry(j)

        @pl.when(own_y & (zz <= z) & (z < 3))
        def _():
            up_copy(q).wait_send()

        @pl.when(own_y & (zz >= z) & (z > 0))
        def _():
            down_copy(q).wait_send()

        @pl.when(own_y)
        def _():
            y_copy(q).wait_send()

        @pl.when(j > 0)
        def _():
            x_copy(q).wait_send()

        core_copy(q, c).wait_send()
        core_x_copy(q, c).wait_send()
        return carry

    lax.fori_loop(0, 8, drain, 0)


def scatter_kernel(
    hid, down_hbm, out, down_v, own, oth, got_c, got_xa, got_ya, got_yb, got_xb, got_up, got_dn,
    load_sem, cs, cr, xas, xar, yas, yar, ybs, ybr, xbs, xbr, ups, upr, dns, dnr,
):
    e, z, y, c, x = place()
    rows = own.shape[1]
    top = rows // 2
    width = own.shape[2]
    half = width // 2
    load = pltpu.make_async_copy(down_hbm.at[0], down_v, load_sem.at[0])
    load.start()
    barrier = pltpu.get_barrier_semaphore()
    peer_c, peer_x, peer_y = dev(z, y, 1 - c, x), dev(z, y, c, 1 - x), dev(z, 1 - y, c, x)
    above, below = dev(jnp.minimum(z + 1, 3), y, c, x), dev(jnp.maximum(z - 1, 0), y, c, x)
    for peer in (peer_c, peer_x, peer_y):
        pl.semaphore_signal(barrier, inc=1, device_id=peer, device_id_type=MESH)

    @pl.when(z < 3)
    def _():
        pl.semaphore_signal(barrier, inc=1, device_id=above, device_id_type=MESH)

    @pl.when(z > 0)
    def _():
        pl.semaphore_signal(barrier, inc=1, device_id=below, device_id_type=MESH)

    pl.semaphore_wait(barrier, jnp.where((z == 0) | (z == 3), 4, 5))
    load.wait()

    keep = pl.ds(pl.multiple_of(x * half, 128), half)
    give = pl.ds(pl.multiple_of((1 - x) * half, 128), half)
    ra, rb = pl.ds(0, top), pl.ds(top, top)

    def rcopy(src, dst, send, recv, target):
        return pltpu.make_async_remote_copy(
            src_ref=src, dst_ref=dst, send_sem=send, recv_sem=recv,
            device_id=target, device_id_type=MESH,
        )

    def core_copy(q):
        return rcopy(oth.at[q], got_c.at[q], cs.at[q], cr.at[q], peer_c)

    def xa_copy(q):
        return rcopy(own.at[q, ra, give], got_xa.at[q], xas.at[q], xar.at[q], peer_x)

    def ya_copy(t, yy):
        return rcopy(own.at[t * 2 + yy, ra, keep], got_ya.at[t], yas.at[t], yar.at[t], peer_y)

    def yb_copy(t, yy):
        return rcopy(own.at[t * 2 + yy, rb], got_yb.at[t], ybs.at[t], ybr.at[t], peer_y)

    def xb_copy(t):
        return rcopy(own.at[t * 2 + y, rb, give], got_xb.at[t], xbs.at[t], xbr.at[t], peer_x)

    def up_copy(t):
        return rcopy(own.at[t * 2 + y, :, keep], got_up.at[t], ups.at[t], upr.at[t], above)

    def dn_copy(t):
        return rcopy(own.at[t * 2 + y, :, keep], got_dn.at[t], dns.at[t], dnr.at[t], below)

    def entry(j):
        t = pick(j // 2, TARGETS)
        return t, jnp.where(j % 2 == 0, 1 - y, y)

    def add(q, r, cols, other):
        own[q, r, cols] = (own[q, r, cols].astype(F32) + other.astype(F32)).astype(BF16)

    def stage_a(j):
        t, yy = entry(j)
        q = t * 2 + yy
        theirs = hid[q * 2 + 1 - c]
        ours = hid[q * 2 + c]
        both = jnp.concatenate([theirs, ours], axis=0)
        for n in range(0, width, 512):
            p = jnp.dot(both, down_v[:, n:n + 512], preferred_element_type=F32).astype(BF16)
            oth[q, :, n:n + 512] = p[:rows]
            own[q, :, n:n + 512] = p[rows:]
        core_copy(q).start()

    def stage_b(j):
        t, yy = entry(j)
        q = t * 2 + yy
        core_copy(q).wait_recv()
        add(q, slice(None), slice(None), got_c[q])
        xa_copy(q).start()

        @pl.when(yy != y)
        def _():
            yb_copy(t, yy).start()

    def stage_c(j):
        t, yy = entry(j)
        q = t * 2 + yy
        xa_copy(q).wait_recv()
        add(q, ra, keep, got_xa[q])

        @pl.when(yy != y)
        def _():
            ya_copy(t, yy).start()

        @pl.when(yy == y)
        def _():
            yb_copy(t, yy).wait_recv()
            add(q, rb, slice(None), got_yb[t])
            xb_copy(t).start()

    def stage_d(i):
        t = pick(i, TARGETS)
        q = t * 2 + y
        ya_copy(t, y).wait_recv()
        add(q, ra, keep, got_ya[t])
        xb_copy(t).wait_recv()
        add(q, rb, keep, got_xb[t])

        @pl.when((t > z) & (z > 0))
        def _():
            up_copy(t).wait_recv()
            add(q, slice(None), keep, got_up[t])

        @pl.when(t > z)
        def _():
            up_copy(t).start()

        @pl.when((t < z) & (z < 3))
        def _():
            dn_copy(t).wait_recv()
            add(q, slice(None), keep, got_dn[t])

        @pl.when(t < z)
        def _():
            dn_copy(t).start()

    def step(j, carry):
        @pl.when(j < 8)
        def _():
            stage_a(j)

        @pl.when((j >= 1) & (j < 9))
        def _():
            stage_b(j - 1)

        @pl.when((j >= 3) & (j < 11))
        def _():
            stage_c(j - 3)

        @pl.when((j >= 6) & (j % 2 == 0))
        def _():
            stage_d((j - 6) // 2)

        return carry

    lax.fori_loop(0, 13, step, 0)

    @pl.when(z > 0)
    def _():
        up_copy(z).wait_recv()
        add(z * 2 + y, slice(None), keep, got_up[z])

    @pl.when(z < 3)
    def _():
        dn_copy(z).wait_recv()
        add(z * 2 + y, slice(None), keep, got_dn[z])

    out[...] = own[z * 2 + y, :, keep]

    def drain(q, carry):
        core_copy(q).wait_send()
        xa_copy(q).wait_send()
        return carry

    lax.fori_loop(0, 8, drain, 0)

    def drain_t(t, carry):
        ya_copy(t, 1 - y).wait_send()
        yb_copy(t, 1 - y).wait_send()
        xb_copy(t).wait_send()

        @pl.when(t > z)
        def _():
            up_copy(t).wait_send()

        @pl.when(t < z)
        def _():
            dn_copy(t).wait_send()

        return carry

    lax.fori_loop(0, 4, drain_t, 0)


def dense_weights(expert_ids, route_weights, experts):
    hit = expert_ids[None] == jnp.arange(experts, dtype=jnp.int32)[:, None, None]
    return jnp.sum(jnp.where(hit, route_weights[None], 0.0), axis=2)


def on_box(tokens, expert_ids, route_weights, gate_w, up_w, down_w):
    rows, width = tokens.shape
    n_dev = lax.axis_size("expert")
    hidden_units = gate_w.shape[2]
    wts = dense_weights(expert_ids, route_weights, n_dev)
    any_ = pl.BlockSpec(memory_space=pl.ANY)
    vmem = pl.BlockSpec(memory_space=pltpu.VMEM)
    sem = lambda *s: pltpu.SemaphoreType.DMA(s)
    half = width // 2
    hid = pl.pallas_call(
        gather_kernel,
        out_shape=jax.ShapeDtypeStruct((n_dev, rows, hidden_units), BF16),
        in_specs=[any_] * 4,
        out_specs=vmem,
        scratch_shapes=[
            pltpu.VMEM((n_dev, rows, width), BF16),
            pltpu.VMEM((width, hidden_units), BF16),
            pltpu.VMEM((width, hidden_units), BF16),
            pltpu.VMEM((n_dev, n_dev, rows), F32),
            sem(2), sem(2), sem(n_dev), sem(n_dev), sem(2, 4), sem(4),
            sem(8), sem(8), sem(8), sem(8), sem(8), sem(8), sem(8),
        ],
        compiler_params=pltpu.CompilerParams(
            collective_id=0, has_side_effects=True, vmem_limit_bytes=60 * 2**20
        ),
        name="gather_up",
    )(tokens, wts, gate_w, up_w)
    big = lambda n, r, w: pltpu.VMEM((n, r, w), BF16)
    return pl.pallas_call(
        scatter_kernel,
        out_shape=jax.ShapeDtypeStruct((rows, half), BF16),
        in_specs=[vmem, any_],
        out_specs=vmem,
        scratch_shapes=[
            pltpu.VMEM((hidden_units, width), BF16),
            big(8, rows, width), big(8, rows, width), big(8, rows, width),
            big(8, rows // 2, half), big(4, rows // 2, half),
            big(4, rows // 2, width), big(4, rows // 2, half),
            big(4, rows, half), big(4, rows, half),
            sem(1), sem(8), sem(8), sem(8), sem(8), sem(4), sem(4), sem(4), sem(4),
            sem(4), sem(4), sem(4), sem(4), sem(4), sem(4),
        ],
        compiler_params=pltpu.CompilerParams(
            collective_id=1, has_side_effects=True, vmem_limit_bytes=62 * 2**20
        ),
        name="down_scatter",
    )(hid, down_w)


def anywhere(tokens, expert_ids, route_weights, gate_w, up_w, down_w):
    rows, width = tokens.shape
    local_experts = gate_w.shape[0]
    experts = local_experts * lax.axis_size("expert")
    first = lax.axis_index("expert") * local_experts
    wts = dense_weights(expert_ids, route_weights, experts)
    every = lax.all_gather(tokens, "expert", axis=0, tiled=True)
    wall = lax.all_gather(wts, "expert", axis=1, tiled=True)
    total = None
    for i in range(local_experts):
        w = lax.dynamic_index_in_dim(wall, first + i, 0, keepdims=False)[:, None]
        g = jnp.dot(every, gate_w[i], preferred_element_type=F32)
        u = jnp.dot(every, up_w[i], preferred_element_type=F32)
        h = (jax.nn.silu(g) * u * w).astype(BF16)
        p = jnp.dot(h, down_w[i], preferred_element_type=F32)
        total = p if total is None else total + p
    mixed = lax.psum_scatter(total.astype(BF16), "expert", scatter_dimension=0, tiled=True)
    return lax.psum_scatter(mixed, "tensor", scatter_dimension=1, tiled=True)


def solution(mesh):
    shape = dict(mesh.shape)
    box = shape == {"groups": 1, "expert": 16, "tensor": 2}
    in_specs = (
        P(("groups", "expert"), None),
        P(("groups", "expert"), None),
        P(("groups", "expert"), None),
        P("expert", None, "tensor"),
        P("expert", None, "tensor"),
        P("expert", "tensor", None),
    )
    out_specs = P(("groups", "expert"), "tensor")
    return jax.shard_map(
        on_box if box else anywhere, mesh=mesh, in_specs=in_specs, out_specs=out_specs, check_vma=False
    )
```

```python
import functools

import jax
import jax.numpy as jnp
from jax import lax
from jax.experimental import pallas as pl
from jax.experimental.pallas import tpu as pltpu
from jax.sharding import PartitionSpec as P

MESH = pl.DeviceIdType.MESH
F32, BF16 = jnp.float32, jnp.bfloat16
ORDER = (
    (0, 2, 1, 4, 3, 6, 5, 7),
    (2, 0, 3, 4, 1, 6, 5, 7),
    (4, 6, 5, 2, 7, 0, 3, 1),
    (6, 4, 7, 2, 5, 0, 3, 1),
)
TARGETS = (3, 0, 2, 1)
X_LAG, UP_LAG = 3, 4
JOIN_LAG, LAST_LAG, CHAIN_LAG = 4, 7, 12


def place():
    e = lax.axis_index("expert")
    return e, e // 4, (e // 2) % 2, e % 2, lax.axis_index("tensor")


def pick(index, values):
    out = jnp.int32(0)
    for k, v in enumerate(values):
        if v:
            out = out + jnp.where(index == k, jnp.int32(v), jnp.int32(0))
    return out


def dev(z, y, c, x):
    return {"expert": (z * 2 + y) * 2 + c, "tensor": x}


def gather_kernel(
    tok, wts, gate_hbm, up_hbm, hid, held, gate_v, up_v, wall,
    own_sem, load_sem, wsend, wrecv, zs, ys, xs, cs, cxs, rp, rx, rc, rcx,
):
    e, z, y, c, x = place()
    n_dev = wall.shape[0]
    rows = held.shape[1]
    lane = 3 * rows // 8
    main = rows - lane
    mine = pl.ds(pl.multiple_of(lane * x, 16), main)
    out_x = pl.ds(pl.multiple_of(main * x, 16), lane)
    in_x = pl.ds(pl.multiple_of(main * (1 - x), 16), lane)
    me_q = z * 2 + y

    load_own = pltpu.make_async_copy(tok, held.at[e], own_sem.at[0])
    load_own.start()
    load_gate = pltpu.make_async_copy(gate_hbm.at[0], gate_v, load_sem.at[0])
    load_up = pltpu.make_async_copy(up_hbm.at[0], up_v, load_sem.at[1])
    load_gate.start()
    load_up.start()
    load_w = pltpu.make_async_copy(wts, wall.at[e], own_sem.at[1])
    load_w.start()

    barrier = pltpu.get_barrier_semaphore()

    def greet(k, carry):
        pl.semaphore_signal(
            barrier, inc=1, device_id={"expert": (e + k) % n_dev, "tensor": x}, device_id_type=MESH
        )
        return carry

    lax.fori_loop(1, n_dev, greet, 0)
    pl.semaphore_signal(barrier, inc=1, device_id=dev(z, y, c, 1 - x), device_id_type=MESH)
    pl.semaphore_wait(barrier, n_dev)

    def cp(q, lane_c, part, send, recv, target):
        ref = held.at[q * 2 + lane_c] if part is None else held.at[q * 2 + lane_c, part]
        return pltpu.make_async_remote_copy(
            src_ref=ref, dst_ref=ref, send_sem=send, recv_sem=recv,
            device_id=target, device_id_type=MESH,
        )

    def up_copy(q):
        return cp(q, c, mine, zs.at[0, q // 2], rp.at[q], dev(jnp.minimum(z + 1, 3), y, c, x))

    def down_copy(q):
        return cp(q, c, mine, zs.at[1, q // 2], rp.at[q], dev(jnp.maximum(z - 1, 0), y, c, x))

    def y_copy(q):
        return cp(q, c, mine, ys.at[q // 2], rp.at[q], dev(z, 1 - y, c, x))

    def x_copy(q):
        return cp(q, c, out_x, xs.at[q], rx.at[q], dev(z, y, c, 1 - x))

    def x_arrive(q):
        return cp(q, c, in_x, xs.at[q], rx.at[q], dev(z, y, c, 1 - x))

    def core_copy(q, lane_c):
        return cp(q, lane_c, mine, cs.at[q], rc.at[q], dev(z, y, 1 - c, x))

    def core_x_copy(q, lane_c):
        return cp(q, lane_c, in_x, cxs.at[q], rcx.at[q], dev(z, y, 1 - c, x))

    def w_copy(k):
        return pltpu.make_async_remote_copy(
            src_ref=wall.at[e], dst_ref=wall.at[e], send_sem=wsend.at[k], recv_sem=wrecv.at[k],
            device_id={"expert": (e + k) % n_dev, "tensor": x}, device_id_type=MESH,
        )

    def w_arrive(k):
        ref = wall.at[(e + n_dev - k) % n_dev]
        return pltpu.make_async_remote_copy(
            src_ref=ref, dst_ref=ref, send_sem=wsend.at[k], recv_sem=wrecv.at[k],
            device_id={"expert": (e + k) % n_dev, "tensor": x}, device_id_type=MESH,
        )

    load_own.wait()

    @pl.when(z < 3)
    def _():
        up_copy(me_q).start()

    @pl.when(z > 0)
    def _():
        down_copy(me_q).start()

    y_copy(me_q).start()
    core_copy(me_q, c).start()
    core_x_copy(me_q, c).start()
    load_w.wait()

    def send_w(k, carry):
        w_copy(k).start()
        return carry

    lax.fori_loop(1, n_dev, send_w, 0)

    def entry(j):
        v = pick(z * 8 + j, [v for row in ORDER for v in row])
        own_y = v % 2 == 0
        return (v // 2) * 2 + jnp.where(own_y, y, 1 - y), v // 2, own_y

    def compute(q):
        a = held[pl.ds(q * 2, 2)].reshape(2 * rows, held.shape[2])
        experts = wall.shape[1]
        col = lax.broadcasted_iota(jnp.int32, (rows, experts), 1) == e
        w0 = jnp.sum(jnp.where(col, wall[q * 2].T, 0.0), axis=1, keepdims=True)
        w1 = jnp.sum(jnp.where(col, wall[q * 2 + 1].T, 0.0), axis=1, keepdims=True)
        w = jnp.concatenate([w0, w1], axis=0)
        for n in range(0, gate_v.shape[1], 256):
            g = jnp.dot(a, gate_v[:, n:n + 256], preferred_element_type=F32)
            u = jnp.dot(a, up_v[:, n:n + 256], preferred_element_type=F32)
            h = (g / (1.0 + jnp.exp(-g)) * u * w).astype(BF16)
            hid[pl.ds(q * 2, 2), :, n:n + 256] = h.reshape(2, rows, 256)

    def step(j, carry):
        @pl.when((j >= 1) & (j < 8))
        def _():
            q, zz, own_y = entry(j)
            y_copy(q).wait_recv()

            @pl.when(own_y & (zz < z) & (z < 3))
            def _():
                up_copy(q).start()

            @pl.when(own_y & (zz > z) & (z > 0))
            def _():
                down_copy(q).start()

            @pl.when(own_y)
            def _():
                y_copy(q).start()

            x_copy(q).start()
            core_copy(q, c).start()

        @pl.when((j >= 1 + X_LAG) & (j < 8 + X_LAG))
        def _():
            q, zz, own_y = entry(j - X_LAG)
            x_arrive(q).wait_recv()
            core_x_copy(q, c).start()

        @pl.when(j == 0)
        def _():
            load_gate.wait()
            load_up.wait()

            def got_w(k, carry):
                w_arrive(k).wait_recv()
                return carry

            lax.fori_loop(1, n_dev, got_w, 0)

        @pl.when((j == 0) | (j >= 1 + UP_LAG))
        def _():
            q, zz, own_y = entry(jnp.where(j == 0, 0, j - UP_LAG))
            core_copy(q, 1 - c).wait_recv()
            core_x_copy(q, 1 - c).wait_recv()
            compute(q)

        return carry

    lax.fori_loop(0, 8 + UP_LAG, step, 0)

    def drain_w(k, carry):
        w_copy(k).wait_send()
        return carry

    lax.fori_loop(1, n_dev, drain_w, 0)

    def drain(j, carry):
        q, zz, own_y = entry(j)

        @pl.when(own_y & (zz <= z) & (z < 3))
        def _():
            up_copy(q).wait_send()

        @pl.when(own_y & (zz >= z) & (z > 0))
        def _():
            down_copy(q).wait_send()

        @pl.when(own_y)
        def _():
            y_copy(q).wait_send()

        @pl.when(j > 0)
        def _():
            x_copy(q).wait_send()

        core_copy(q, c).wait_send()
        core_x_copy(q, c).wait_send()
        return carry

    lax.fori_loop(0, 8, drain, 0)


def scatter_kernel(
    hid, down_hbm, out, down_v, own, oth, got_c, got_xa, got_ya, got_yb, got_xb, got_up, got_dn,
    load_sem, cs, cr, xas, xar, yas, yar, ybs, ybr, xbs, xbr, ups, upr, dns, dnr,
):
    e, z, y, c, x = place()
    rows = own.shape[1]
    top = rows // 2
    width = own.shape[2]
    half = width // 2
    load = pltpu.make_async_copy(down_hbm.at[0], down_v, load_sem.at[0])
    load.start()
    barrier = pltpu.get_barrier_semaphore()
    peer_c, peer_x, peer_y = dev(z, y, 1 - c, x), dev(z, y, c, 1 - x), dev(z, 1 - y, c, x)
    above, below = dev(jnp.minimum(z + 1, 3), y, c, x), dev(jnp.maximum(z - 1, 0), y, c, x)
    for peer in (peer_c, peer_x, peer_y):
        pl.semaphore_signal(barrier, inc=1, device_id=peer, device_id_type=MESH)

    @pl.when(z < 3)
    def _():
        pl.semaphore_signal(barrier, inc=1, device_id=above, device_id_type=MESH)

    @pl.when(z > 0)
    def _():
        pl.semaphore_signal(barrier, inc=1, device_id=below, device_id_type=MESH)

    pl.semaphore_wait(barrier, jnp.where((z == 0) | (z == 3), 4, 5))
    load.wait()

    keep = pl.ds(pl.multiple_of(x * half, 128), half)
    give = pl.ds(pl.multiple_of((1 - x) * half, 128), half)
    ra, rb = pl.ds(0, top), pl.ds(top, top)

    def rcopy(src, dst, send, recv, target):
        return pltpu.make_async_remote_copy(
            src_ref=src, dst_ref=dst, send_sem=send, recv_sem=recv,
            device_id=target, device_id_type=MESH,
        )

    def core_copy(q):
        return rcopy(oth.at[q], got_c.at[q], cs.at[q], cr.at[q], peer_c)

    def xa_copy(q):
        return rcopy(own.at[q, ra, give], got_xa.at[q], xas.at[q], xar.at[q], peer_x)

    def ya_copy(t, yy):
        return rcopy(own.at[t * 2 + yy, ra, keep], got_ya.at[t], yas.at[t], yar.at[t], peer_y)

    def yb_copy(t, yy):
        return rcopy(own.at[t * 2 + yy, rb], got_yb.at[t], ybs.at[t], ybr.at[t], peer_y)

    def xb_copy(t):
        return rcopy(own.at[t * 2 + y, rb, give], got_xb.at[t], xbs.at[t], xbr.at[t], peer_x)

    def up_copy(t):
        return rcopy(own.at[t * 2 + y, :, keep], got_up.at[t], ups.at[t], upr.at[t], above)

    def dn_copy(t):
        return rcopy(own.at[t * 2 + y, :, keep], got_dn.at[t], dns.at[t], dnr.at[t], below)

    def entry(j):
        t = pick(j // 2, TARGETS)
        return t, jnp.where(j % 2 == 0, 1 - y, y)

    def add(q, r, cols, other):
        own[q, r, cols] = (own[q, r, cols].astype(F32) + other.astype(F32)).astype(BF16)

    def stage_a(j):
        t, yy = entry(j)
        q = t * 2 + yy
        theirs = hid[q * 2 + 1 - c]
        ours = hid[q * 2 + c]
        both = jnp.concatenate([theirs, ours], axis=0)
        for n in range(0, width, 512):
            p = jnp.dot(both, down_v[:, n:n + 512], preferred_element_type=F32).astype(BF16)
            oth[q, :, n:n + 512] = p[:rows]
            own[q, :, n:n + 512] = p[rows:]
        core_copy(q).start()

    def stage_b(j):
        t, yy = entry(j)
        q = t * 2 + yy
        core_copy(q).wait_recv()
        add(q, slice(None), slice(None), got_c[q])
        xa_copy(q).start()

        @pl.when(yy != y)
        def _():
            yb_copy(t, yy).start()

    def stage_c(j):
        t, yy = entry(j)
        q = t * 2 + yy
        xa_copy(q).wait_recv()
        add(q, ra, keep, got_xa[q])

        @pl.when(yy != y)
        def _():
            ya_copy(t, yy).start()

        @pl.when(yy == y)
        def _():
            yb_copy(t, yy).wait_recv()
            add(q, rb, slice(None), got_yb[t])
            xb_copy(t).start()

    def stage_d(i):
        t = pick(i, TARGETS)
        q = t * 2 + y
        ya_copy(t, y).wait_recv()
        add(q, ra, keep, got_ya[t])
        xb_copy(t).wait_recv()
        add(q, rb, keep, got_xb[t])

        @pl.when((t > z) & (z == 0))
        def _():
            up_copy(t).start()

        @pl.when((t < z) & (z == 3))
        def _():
            dn_copy(t).start()

    def stage_e(i):
        t = pick(i, TARGETS)
        q = t * 2 + y

        @pl.when((t > z) & (z > 0))
        def _():
            up_copy(t).wait_recv()
            add(q, slice(None), keep, got_up[t])
            up_copy(t).start()

        @pl.when((t < z) & (z < 3))
        def _():
            dn_copy(t).wait_recv()
            add(q, slice(None), keep, got_dn[t])
            dn_copy(t).start()

    def step(j, carry):
        @pl.when(j < 8)
        def _():
            stage_a(j)

        @pl.when((j >= 1) & (j < 9))
        def _():
            stage_b(j - 1)

        @pl.when((j >= JOIN_LAG) & (j < 8 + JOIN_LAG))
        def _():
            stage_c(j - JOIN_LAG)

        @pl.when((j >= LAST_LAG) & (j < 8 + LAST_LAG) & ((j - LAST_LAG) % 2 == 0))
        def _():
            stage_d((j - LAST_LAG) // 2)

        @pl.when((j >= CHAIN_LAG) & ((j - CHAIN_LAG) % 2 == 0))
        def _():
            stage_e((j - CHAIN_LAG) // 2)

        return carry

    lax.fori_loop(0, 7 + CHAIN_LAG, step, 0)

    @pl.when(z > 0)
    def _():
        up_copy(z).wait_recv()
        add(z * 2 + y, slice(None), keep, got_up[z])

    @pl.when(z < 3)
    def _():
        dn_copy(z).wait_recv()
        add(z * 2 + y, slice(None), keep, got_dn[z])

    out[...] = own[z * 2 + y, :, keep]

    def drain(q, carry):
        core_copy(q).wait_send()
        xa_copy(q).wait_send()
        return carry

    lax.fori_loop(0, 8, drain, 0)

    def drain_t(t, carry):
        ya_copy(t, 1 - y).wait_send()
        yb_copy(t, 1 - y).wait_send()
        xb_copy(t).wait_send()

        @pl.when(t > z)
        def _():
            up_copy(t).wait_send()

        @pl.when(t < z)
        def _():
            dn_copy(t).wait_send()

        return carry

    lax.fori_loop(0, 4, drain_t, 0)


def dense_weights(expert_ids, route_weights, experts):
    hit = expert_ids[None] == jnp.arange(experts, dtype=jnp.int32)[:, None, None]
    return jnp.sum(jnp.where(hit, route_weights[None], 0.0), axis=2)


def on_box(tokens, expert_ids, route_weights, gate_w, up_w, down_w):
    rows, width = tokens.shape
    n_dev = lax.axis_size("expert")
    hidden_units = gate_w.shape[2]
    wts = dense_weights(expert_ids, route_weights, n_dev)
    any_ = pl.BlockSpec(memory_space=pl.ANY)
    vmem = pl.BlockSpec(memory_space=pltpu.VMEM)
    sem = lambda *s: pltpu.SemaphoreType.DMA(s)
    half = width // 2
    hid = pl.pallas_call(
        gather_kernel,
        out_shape=jax.ShapeDtypeStruct((n_dev, rows, hidden_units), BF16),
        in_specs=[any_] * 4,
        out_specs=vmem,
        scratch_shapes=[
            pltpu.VMEM((n_dev, rows, width), BF16),
            pltpu.VMEM((width, hidden_units), BF16),
            pltpu.VMEM((width, hidden_units), BF16),
            pltpu.VMEM((n_dev, n_dev, rows), F32),
            sem(2), sem(2), sem(n_dev), sem(n_dev), sem(2, 4), sem(4),
            sem(8), sem(8), sem(8), sem(8), sem(8), sem(8), sem(8),
        ],
        compiler_params=pltpu.CompilerParams(
            collective_id=0, has_side_effects=True, vmem_limit_bytes=60 * 2**20
        ),
        name="gather_up",
    )(tokens, wts, gate_w, up_w)
    big = lambda n, r, w: pltpu.VMEM((n, r, w), BF16)
    return pl.pallas_call(
        scatter_kernel,
        out_shape=jax.ShapeDtypeStruct((rows, half), BF16),
        in_specs=[vmem, any_],
        out_specs=vmem,
        scratch_shapes=[
            pltpu.VMEM((hidden_units, width), BF16),
            big(8, rows, width), big(8, rows, width), big(8, rows, width),
            big(8, rows // 2, half), big(4, rows // 2, half),
            big(4, rows // 2, width), big(4, rows // 2, half),
            big(4, rows, half), big(4, rows, half),
            sem(1), sem(8), sem(8), sem(8), sem(8), sem(4), sem(4), sem(4), sem(4),
            sem(4), sem(4), sem(4), sem(4), sem(4), sem(4),
        ],
        compiler_params=pltpu.CompilerParams(
            collective_id=1, has_side_effects=True, vmem_limit_bytes=62 * 2**20
        ),
        name="down_scatter",
    )(hid, down_w)


def anywhere(tokens, expert_ids, route_weights, gate_w, up_w, down_w):
    rows, width = tokens.shape
    local_experts = gate_w.shape[0]
    experts = local_experts * lax.axis_size("expert")
    first = lax.axis_index("expert") * local_experts
    wts = dense_weights(expert_ids, route_weights, experts)
    every = lax.all_gather(tokens, "expert", axis=0, tiled=True)
    wall = lax.all_gather(wts, "expert", axis=1, tiled=True)
    total = None
    for i in range(local_experts):
        w = lax.dynamic_index_in_dim(wall, first + i, 0, keepdims=False)[:, None]
        g = jnp.dot(every, gate_w[i], preferred_element_type=F32)
        u = jnp.dot(every, up_w[i], preferred_element_type=F32)
        h = (jax.nn.silu(g) * u * w).astype(BF16)
        p = jnp.dot(h, down_w[i], preferred_element_type=F32)
        total = p if total is None else total + p
    mixed = lax.psum_scatter(total.astype(BF16), "expert", scatter_dimension=0, tiled=True)
    return lax.psum_scatter(mixed, "tensor", scatter_dimension=1, tiled=True)


def solution(mesh):
    shape = dict(mesh.shape)
    box = shape == {"groups": 1, "expert": 16, "tensor": 2}
    in_specs = (
        P(("groups", "expert"), None),
        P(("groups", "expert"), None),
        P(("groups", "expert"), None),
        P("expert", None, "tensor"),
        P("expert", None, "tensor"),
        P("expert", "tensor", None),
    )
    out_specs = P(("groups", "expert"), "tensor")
    return jax.shard_map(
        on_box if box else anywhere, mesh=mesh, in_specs=in_specs, out_specs=out_specs, check_vma=False
    )
```
